256 devices in a mesh: bulk: 16 (over x, y), grp: 16 (over z, core).
Axes of the slice: x: 4, y: 4, z: 8, core: 2. Of those that a mesh axis runs over, the one named last changes fastest.
Arguments:
- embeddings: bfloat16 [131072, 768], P(('bulk', 'grp')), may hold values from -6 to 6
- cluster_ids: int32 [131072, 1], P(('bulk', 'grp')), may hold values from 0 to 15; in each aligned block of 512 rows (0 to 511, 512 to 1023, ...) at most 48 rows name the same one
- row_order: int32 [131072], P(('bulk', 'grp')), may hold values from 0 to 131071, each once
Outputs:
- earlier_max: float32 [131072], P(('bulk', 'grp'))
The draws below stay inside these ranges and needn't reach their ends.
Inputs may be any that keep to these rules, and one draw needn't show every extreme that they name: `cluster_ids`: the rows of one device name any one cluster at most 48 times; some cluster is named exactly 48 times by some device's rows.
All inputs are finite; a program needn't handle non-finite values.
Results may differ from the reference program's by a relative error of at most 0.0013.
Values may be sent and summed in bfloat16 or wider, within the bound.
A program may use at most 64 MiB of HBM per device.

```python
import math
import jax
import jax.numpy as jnp
import numpy as np
from jax import lax

D = 768
ROWS_DEV = 512
CAP = 48
CLUSTERS = 16
ROWS = 131072
N_BULK = 16
N_GRP = 16


def levels(key, shape, cuts, smallest, high):
    gain = 1.0
    for dim, shards_of in cuts:
        heights = jax.random.uniform(jax.random.fold_in(jax.random.fold_in(key, 6), dim), (shards_of,), jnp.float32, smallest / len(cuts), high / len(cuts))
        gain = gain * jnp.repeat(jnp.exp(heights), shape[dim] // shards_of).reshape((-1,) + (1,) * (len(shape) - 1 - dim))
    return gain


def deal_out(own_key, own, number, rows, number_of, top, reach, skew):
    sequence = jax.random.permutation(own_key, number_of)
    packed, ordinary = portions_of(number_of, rows * top, reach, skew, True), portions_of(number_of, rows * top, reach, skew, False)
    places = jnp.arange(number_of)

    def named(lengths, turn):
        used = int((lengths > 0).sum())
        fixed = max(1, used // 4)
        passed = fixed + (places - fixed + turn * (used - fixed)) % max(1, number_of - fixed)
        return jnp.zeros((number_of,), jnp.int32).at[sequence[jnp.where(places < fixed, places, passed)]].set(jnp.asarray(lengths, jnp.int32))

    lengths = jnp.where(number % 4 == 0, named(packed, number // 4), named(ordinary, number - number // 4 - 1))
    mixed = jax.random.permutation(jax.random.fold_in(own, 3), number_of)
    giver, receiver = mixed[0:number_of // 2 * 2:2], mixed[1:number_of // 2 * 2:2]
    slack = jnp.minimum(lengths[giver] - 1, reach - lengths[receiver]) // 2
    slack = jnp.where((giver == sequence[0]) | (receiver == sequence[0]) | (lengths[receiver] == 0), 0, jnp.maximum(slack, 0))
    passed = jax.random.randint(jax.random.fold_in(own, 4), (number_of // 2,), 0, 1 << 20) % (slack + 1)
    lengths = lengths.at[giver].add(-passed).at[receiver].add(passed)
    items = jnp.searchsorted(jnp.cumsum(lengths), jnp.arange(rows * top), side="right").astype(jnp.int32)
    listing = items.reshape(top, rows).T
    listing = listing[jax.random.permutation(jax.random.fold_in(own, 1), rows)]
    turn = jax.random.randint(jax.random.fold_in(own, 2), (rows, 1), 0, top)
    return jnp.take_along_axis(listing, (jnp.arange(top)[None, :] + turn) % top, axis=1)


def portions_of(count, total, bound, lean, full):
    weights = [(1 << 20) // math.isqrt(grade ** lean) + 1 for grade in range(1, count + 1)]
    largest = bound if full else min(bound, max(-(-total // count), total * weights[0] // sum(weights)))
    least = 1 if total - largest >= count - 1 else 0
    given, spare = [largest] + [least] * (count - 1), total - largest - least * (count - 1)
    while spare > 0:
        movable = [i for i in range(1, count) if given[i] < largest] or [i for i in range(1, count) if given[i] < bound]
        mass, left = sum([weights[i] for i in movable]), spare
        for i in movable:
            extra = min(bound - given[i], max(1, left * weights[i] // mass), spare)
            given[i] = given[i] + extra
            spare = spare - extra
    return np.array(given)


def noise(stream_key, extent, spread, limit, shards=(), kind=jnp.bfloat16):
    drawn = jax.random.normal(stream_key, extent, jnp.float32) * spread
    if len(shards) > 0:
        drawn = levels(stream_key, extent, shards, -0.22, 0.18) * drawn
    return jnp.clip(drawn, min=-limit, max=limit).astype(kind)


def setup_inputs(seed: int = 0) -> dict:
    keys = jax.random.split(jax.random.key(seed), 4)
    embeddings = noise(keys[0], (ROWS, D), 1.0, 6.0, ((0, 256),))
    cluster_ids_keys = jax.random.split(jax.random.fold_in(keys[1], 1), ROWS // ROWS_DEV)
    cluster_ids_turns = jax.random.permutation(jax.random.fold_in(keys[1], 3), ROWS // ROWS_DEV)
    cluster_ids = jax.vmap(lambda own, number: deal_out(jax.random.fold_in(keys[1], 2), own, number, ROWS_DEV, CLUSTERS, 1, CAP, 2))(cluster_ids_keys, cluster_ids_turns).reshape((ROWS, 1))
    row_order = jax.random.permutation(keys[2], ROWS).astype(jnp.int32)
    return dict(embeddings=embeddings, cluster_ids=cluster_ids, row_order=row_order)


def reference(embeddings, cluster_ids, row_order):
    values = embeddings.astype(jnp.float32)
    unit = (values * lax.rsqrt(lax.optimization_barrier(jnp.sum(values * values, axis=1, keepdims=True)) + 1e-06)).astype(jnp.bfloat16)
    total = embeddings.shape[0]
    cluster = cluster_ids[:, 0].astype(jnp.int32)
    keyed = cluster * total + row_order.astype(jnp.int32)
    permuted = jnp.argsort(keyed).astype(jnp.int32)
    sorted_unit = unit[permuted]
    sorted_cluster = cluster[permuted]
    counts = lax.optimization_barrier(jnp.sum((cluster[:, None] == jnp.arange(N_BULK, dtype=jnp.int32)[None, :]).astype(jnp.int32), axis=0))
    starts = (jnp.cumsum(counts) - counts).astype(jnp.int32)
    biggest = N_BULK * N_GRP * CAP
    padded = jnp.concatenate([sorted_unit, jnp.zeros((biggest, sorted_unit.shape[1]), jnp.bfloat16)], axis=0)
    places = jnp.arange(biggest, dtype=jnp.int32)

    def one_cluster(index):
        block = lax.dynamic_slice_in_dim(padded, starts[index].astype(jnp.int32), biggest, 0)
        gram = jnp.dot(block, block.T, preferred_element_type=jnp.float32)
        usable = (places[None, :] < places[:, None]) & (places[None, :] < counts[index])
        return lax.optimization_barrier(jnp.max(jnp.where(usable, gram, jnp.float32(-1.0)), axis=1))
    bests = lax.map(one_cluster, jnp.arange(N_BULK, dtype=jnp.int32))
    position = jnp.arange(total, dtype=jnp.int32) - starts[sorted_cluster]
    sorted_result = bests[sorted_cluster, position]
    return jnp.zeros((total,), jnp.float32).at[permuted].set(sorted_result)
```

```python
import functools

import jax
import jax.numpy as jnp
from jax import lax
from jax.experimental import pallas as pl
from jax.experimental.pallas import tpu as pltpu
from jax.sharding import PartitionSpec as P

CAP = 48
NX, NY, NZ = 4, 4, 8
N = 16
S = N * CAP
ROWS = 512
D = 768
BIG = 1e9
LAG = 1
F32 = jnp.float32
BF16 = jnp.bfloat16


def diag():
    return lax.broadcasted_iota(jnp.int32, (CAP, 128), 0) == lax.broadcasted_iota(jnp.int32, (CAP, 128), 1)


def to_rows(column):
    parts = column.reshape(N, CAP, 128)
    return jnp.max(jnp.where(diag()[None], parts, F32(-BIG)), axis=1)


def to_column(rows):
    parts = jnp.broadcast_to(rows[:, None, :], (N, CAP, 128))
    value = jnp.max(jnp.where(diag()[None], parts, F32(-BIG)), axis=2, keepdims=True)
    return jnp.broadcast_to(value, (N, CAP, 128)).reshape(S, 128)


def chunk(n):
    return pl.ds(pl.multiple_of(n * CAP, 16), CAP)


def kernel(emb, cluster, order, out,
           send, buf, slot, osend, orecv, oblk, ocol, olane, rowacc, colacc, res, rrecv, fsend, fin,
           local, d_send, d_recv, oc_send, oc_recv, ob_send, ob_recv, r_send, r_recv, f_send, f_recv):
    bulk, grp = lax.axis_index("bulk"), lax.axis_index("grp")
    x, y = bulk // NY, bulk % NY
    z, k = grp // 2, grp % 2
    sgn = 1 - 2 * k

    def dev(xx, yy, zz, kk):
        return (xx % NX) * NY + yy, zz * 2 + kk

    def remote(src, dst, s_sem, r_sem, target):
        return pltpu.make_async_remote_copy(
            src_ref=src, dst_ref=dst, send_sem=s_sem, recv_sem=r_sem,
            device_id=target, device_id_type=pl.DeviceIdType.MESH)

    x_one = dev(x + sgn + NX, y, z, k)
    mate_y = y + 1 - 2 * (y % 2)
    partner = dev(x, y, z, 1 - k)
    homes = [
        None,
        dev(x - sgn + NX, y, z, k),
        dev(x + 2, y, z, k),
        dev(x + 2 * k, mate_y, z, k),
        partner,
        dev(x + sgn + NX, y, z, 1 - k),
    ]
    users = [
        None,
        x_one,
        dev(x + 2, y, z, k),
        dev(x + 2 * k, mate_y, z, k),
        partner,
        dev(x + sgn + NX, y, z, 1 - k),
    ]
    users[5] = dev(x + sgn + NX, y, z, 1 - k)

    def route(n):
        i, half = n // 2, n % 2
        dz = (i % 2) * ((i + 1) // 2) + (1 - i % 2) * (NZ - i // 2)
        yy = half * (NY - 1 - y) + (1 - half) * y
        zz = (z + dz) % NZ
        return dev(x, yy, zz, k), (yy // 2) * NZ + zz, dev(x, yy, (z - dz + 2 * NZ) % NZ, k)

    barrier = pltpu.get_barrier_semaphore()

    def greet(n, carry):
        pl.semaphore_signal(barrier, inc=1, device_id=route(n)[0], device_id_type=pl.DeviceIdType.MESH)
        return carry

    lax.fori_loop(1, N, greet, 0)
    for target in (dev(x + 1, y, z, k), dev(x + 3, y, z, k), dev(x + 2, y, z, k), partner,
                   dev(x + 1, y, z, 1 - k), dev(x + 3, y, z, 1 - k), dev(x, mate_y, z, k), dev(x + 2, mate_y, z, k)):
        pl.semaphore_signal(barrier, inc=1, device_id=target, device_id_type=pl.DeviceIdType.MESH)

    values = emb[...].astype(F32)
    unit = (values * lax.rsqrt(jnp.sum(values * values, axis=1, keepdims=True) + 1e-06)).astype(BF16)
    lane = cluster[...]
    member = lax.broadcasted_iota(jnp.int32, (N, ROWS), 0) == lane
    upper = lax.broadcasted_iota(jnp.int32, (ROWS, ROWS), 0) < lax.broadcasted_iota(jnp.int32, (ROWS, ROWS), 1)
    before = lax.dot_general(
        member.astype(F32).astype(BF16), upper.astype(F32).astype(BF16), (((1,), (0,)), ((), ())),
        preferred_element_type=F32)
    rank = jnp.sum(jnp.where(member, before, F32(0.0)), axis=0, keepdims=True)
    slot[...] = jnp.broadcast_to(lane.astype(F32) * CAP + rank, (8, ROWS))
    orders = order[...].astype(F32)

    def place(begin, size):
        index = lax.broadcasted_iota(jnp.int32, (size, ROWS), 0).astype(F32) + F32(begin)
        return index == slot[0:1, :]

    ocols = []
    for t in range(4):
        hit = place(t * 192, 192)
        send[t * 192:(t + 1) * 192, :] = lax.dot_general(
            hit.astype(F32).astype(BF16), unit, (((1,), (0,)), ((), ())), preferred_element_type=F32).astype(BF16)
        ocols.append(jnp.broadcast_to(
            jnp.min(jnp.where(hit, orders, F32(BIG)), axis=1, keepdims=True), (192, 128)))
    osend[...] = jnp.broadcast_to(to_rows(jnp.concatenate(ocols, axis=0))[:, None, :], (N, 8, 128))
    rowacc[...] = jnp.full((6, S, 128), -1.0, F32)
    colacc[...] = jnp.full((6, 8, S), -1.0, F32)

    pl.semaphore_wait(barrier, N - 1 + 8)

    mine = (y // 2) * NZ + z
    own_rows = pltpu.make_async_copy(send.at[chunk(mine)], buf.at[0, chunk(0)], d_recv.at[0, 0])
    own_rows.start()
    own_order = pltpu.make_async_copy(osend.at[mine], orecv.at[0], local.at[0])
    own_order.start()

    def deal_orders(n, carry):
        target, c, _ = route(n)
        remote(osend.at[c], orecv.at[n], oc_send, oc_recv, target).start()
        return carry

    lax.fori_loop(1, N, deal_orders, 0)

    def deal_rows(n, carry):
        target, c, _ = route(n)
        remote(send.at[chunk(c)], buf.at[0, chunk(n)], d_send.at[0], d_recv.at[0, n], target).start()
        return carry

    lax.fori_loop(1, N, deal_rows, 0)

    def relay(source, n, block, target):
        return remote(buf.at[source, chunk(n)], buf.at[block, chunk(n)], d_send.at[block], d_recv.at[block, n], target)

    def arrived(block, n):
        pltpu.make_async_copy(buf.at[block, chunk(n)], buf.at[block, chunk(n)], d_recv.at[block, n]).wait()

    own_order.wait()
    all_but_one = pl.ds(1, N - 1)
    remote(osend.at[all_but_one], orecv.at[all_but_one], oc_send, oc_recv, partner).wait()
    oblk[0] = jnp.max(orecv[...], axis=1)

    def step(n, carry):
        @pl.when(n < N)
        def _():
            arrived(0, n)
            relay(0, n, 1, users[1]).start()
            relay(0, n, 4, users[4]).start()

        @pl.when(jnp.logical_and(n >= LAG, n < N + LAG))
        def _():
            m = n - LAG
            arrived(1, m)
            relay(1, m, 2, users[1]).start()
            relay(1, m, 5, users[4]).start()

        @pl.when(n >= 2 * LAG)
        def _():
            m = n - 2 * LAG
            arrived(2, m)
            relay(2 * k, m, 3, dev(x, mate_y, z, k)).start()

        return carry

    for b in range(1, 6):
        remote(oblk.at[0], oblk.at[b], ob_send.at[b], ob_recv.at[b], users[b]).start()
    lax.fori_loop(0, N + 2 * LAG, step, 0)
    for b in range(1, 6):
        remote(oblk.at[0], oblk.at[b], ob_send.at[b], ob_recv.at[b], users[b]).wait()

    def spread_orders(b, carry):
        column = to_column(oblk[b])
        ocol[b] = column
        olane[b] = jnp.transpose(column)[0:8, :]
        return carry

    lax.fori_loop(0, 6, spread_orders, 0)
    for b in range(3, 6):
        def drain(n, carry, b=b):
            arrived(b, n)
            return carry

        lax.fori_loop(0, N, drain, 0)

    def tile(i, j, c):
        cols = pl.ds(pl.multiple_of(c * 256, 256), 256)
        score = lax.dot_general(
            buf[i], buf[j, cols, :], (((1,), (1,)), ((), ())), preferred_element_type=F32)
        earlier = olane[j, 0:1, cols] < jnp.concatenate([ocol[i]] * 2, axis=1)
        return cols, score, earlier

    def self_tile(c, carry):
        _, score, earlier = tile(0, 0, c)
        seen = jnp.where(earlier, score, F32(-1.0))
        rowacc[0] = jnp.maximum(rowacc[0], jnp.maximum(seen[:, 0:128], seen[:, 128:256]))
        return carry

    lax.fori_loop(0, 3, self_tile, 0)

    def pair_tile(t, carry):
        u, c = t // 3, t % 3
        g1, g2 = (u + 5) // 7, u // 7
        i = 3 * (g1 - g2) + (2 + 2 * k) * g2
        j = (1 - g1) * (1 + u) + (g1 - g2) * (u - 3 + (u + 1) // 3) + g2 * (u - 3 - 4 * k)
        cols, score, earlier = tile(i, j, c)
        seen = jnp.where(earlier, score, F32(-1.0))
        rowacc[i] = jnp.maximum(rowacc[i], jnp.maximum(seen[:, 0:128], seen[:, 128:256]))
        other = jnp.where(earlier, F32(-1.0), score)
        colacc[j, :, cols] = jnp.maximum(colacc[j, :, cols], jnp.max(other.reshape(S // 8, 8, 256), axis=0))
        return carry

    lax.fori_loop(0, 27, pair_tile, 0)

    def collect(b, carry):
        column = jnp.max(rowacc[b], axis=1, keepdims=True)
        line = jnp.max(colacc[b], axis=0, keepdims=True)
        both = jnp.maximum(column, jnp.transpose(jnp.broadcast_to(line, (128, S))))
        res[b] = to_rows(both)
        return carry

    lax.fori_loop(0, 6, collect, 0)
    for b in range(1, 6):
        remote(res.at[b], rrecv.at[b], r_send.at[b], r_recv.at[b], homes[b]).start()
    rrecv[0] = res[0]
    for b in range(1, 6):
        remote(res.at[b], rrecv.at[b], r_send.at[b], r_recv.at[b], homes[b]).wait()
    best = jnp.max(rrecv[...], axis=0)
    fsend[...] = jnp.broadcast_to(best[:, None, :], (N, 8, 128))

    own_best = pltpu.make_async_copy(fsend.at[0], fin.at[mine], local.at[1])
    own_best.start()

    def give_back(n, carry):
        remote(fsend.at[n], fin.at[mine], f_send, f_recv, route(n)[2]).start()
        return carry

    lax.fori_loop(1, N, give_back, 0)
    remote(buf.at[0, pl.ds(0, S - CAP)], buf.at[0, pl.ds(0, S - CAP)], d_send.at[0], d_recv.at[0, 0], partner).wait_send()
    for b in range(1, 6):
        remote(buf.at[b], buf.at[b], d_send.at[b], d_recv.at[b, 0], partner).wait_send()
    own_best.wait()
    remote(fsend.at[all_but_one], fin.at[all_but_one], f_send, f_recv, partner).wait()
    column = to_column(jnp.max(fin[...], axis=1))
    total = jnp.full((8, ROWS), -BIG, F32)
    for t in range(4):
        hit = place(t * 192, 192)
        part = jnp.where(hit, jnp.concatenate([column[t * 192:(t + 1) * 192, :]] * 4, axis=1), F32(-BIG))
        total = jnp.maximum(total, jnp.max(part.reshape(24, 8, ROWS), axis=0))
    out[...] = jnp.max(total, axis=0, keepdims=True)


def on_device(embeddings, cluster_ids, row_order):
    vmem = pl.BlockSpec(memory_space=pltpu.VMEM)
    dma = pltpu.SemaphoreType.DMA
    result = pl.pallas_call(
        kernel,
        out_shape=jax.ShapeDtypeStruct((1, ROWS), F32),
        in_specs=[vmem] * 3,
        out_specs=vmem,
        scratch_shapes=[
            pltpu.VMEM((S, D), BF16),
            pltpu.VMEM((6, S, D), BF16),
            pltpu.VMEM((8, ROWS), F32),
            pltpu.VMEM((N, 8, 128), F32),
            pltpu.VMEM((N, 8, 128), F32),
            pltpu.VMEM((6, N, 128), F32),
            pltpu.VMEM((6, S, 128), F32),
            pltpu.VMEM((6, 8, S), F32),
            pltpu.VMEM((6, S, 128), F32),
            pltpu.VMEM((6, 8, S), F32),
            pltpu.VMEM((6, N, 128), F32),
            pltpu.VMEM((6, N, 128), F32),
            pltpu.VMEM((N, 8, 128), F32),
            pltpu.VMEM((N, 8, 128), F32),
            dma((2,)), dma((6,)), dma((6, N)), dma, dma, dma((6,)), dma((6,)), dma((6,)), dma((6,)), dma, dma,
        ],
        compiler_params=pltpu.CompilerParams(
            collective_id=0, has_side_effects=True, vmem_limit_bytes=60 * 1024 * 1024),
    )(embeddings, cluster_ids.reshape(1, ROWS), row_order.reshape(1, ROWS))
    return result.reshape(ROWS)


def solution(mesh):
    spec = P(("bulk", "grp"))
    return jax.shard_map(
        on_device,
        mesh=mesh,
        in_specs=(P(("bulk", "grp"), None), P(("bulk", "grp"), None), spec),
        out_specs=spec,
        check_vma=False,
    )
```

```python
import functools

import jax
import jax.numpy as jnp
from jax import lax
from jax.experimental import pallas as pl
from jax.experimental.pallas import tpu as pltpu
from jax.sharding import PartitionSpec as P

CAP = 48
NX, NY, NZ = 4, 4, 8
N = 16
S = N * CAP
ROWS = 512
D = 768
BIG = 1e9
LAG = 2
F32 = jnp.float32
BF16 = jnp.bfloat16


def diag():
    return lax.broadcasted_iota(jnp.int32, (CAP, 128), 0) == lax.broadcasted_iota(jnp.int32, (CAP, 128), 1)


def to_rows(column):
    parts = column.reshape(N, CAP, 128)
    return jnp.max(jnp.where(diag()[None], parts, F32(-BIG)), axis=1)


def to_column(rows):
    parts = jnp.broadcast_to(rows[:, None, :], (N, CAP, 128))
    value = jnp.max(jnp.where(diag()[None], parts, F32(-BIG)), axis=2, keepdims=True)
    return jnp.broadcast_to(value, (N, CAP, 128)).reshape(S, 128)


def chunk(n):
    return pl.ds(pl.multiple_of(n * CAP, 16), CAP)


def kernel(emb, cluster, order, out,
           send, buf, slot, osend, orecv, oblk, ocol, olane, rowacc, colacc, res, rrecv, fsend, fin,
           mid, local, m_send, m_recv, d_send, d_recv, oc_send, oc_recv, ob_send, ob_recv, r_send, r_recv, f_send, f_recv):
    bulk, grp = lax.axis_index("bulk"), lax.axis_index("grp")
    x, y = bulk // NY, bulk % NY
    z, k = grp // 2, grp % 2
    sgn = 1 - 2 * k

    def dev(xx, yy, zz, kk):
        return (xx % NX) * NY + yy, zz * 2 + kk

    def remote(src, dst, s_sem, r_sem, target):
        return pltpu.make_async_remote_copy(
            src_ref=src, dst_ref=dst, send_sem=s_sem, recv_sem=r_sem,
            device_id=target, device_id_type=pl.DeviceIdType.MESH)

    x_one = dev(x + sgn + NX, y, z, k)
    mate_y = y + 1 - 2 * (y % 2)
    partner = dev(x, y, z, 1 - k)
    homes = [
        None,
        dev(x - sgn + NX, y, z, k),
        dev(x + 2, y, z, k),
        dev(x + 2 * k, mate_y, z, k),
        partner,
        dev(x + sgn + NX, y, z, 1 - k),
    ]
    users = [
        None,
        x_one,
        dev(x + 2, y, z, k),
        dev(x + 2 * k, mate_y, z, k),
        partner,
        dev(x + sgn + NX, y, z, 1 - k),
    ]

    def route(n):
        i, half = n // 2, n % 2
        dz = (i % 2) * ((i + 1) // 2) + (1 - i % 2) * (NZ - i // 2)
        yy = half * (NY - 1 - y) + (1 - half) * y
        zz = (z + dz) % NZ
        return dev(x, yy, zz, k), (yy // 2) * NZ + zz, dev(x, yy, (z - dz + 2 * NZ) % NZ, k)

    barrier = pltpu.get_barrier_semaphore()

    def greet(n, carry):
        pl.semaphore_signal(barrier, inc=1, device_id=route(n)[0], device_id_type=pl.DeviceIdType.MESH)
        return carry

    lax.fori_loop(1, N, greet, 0)
    for target in (dev(x + 1, y, z, k), dev(x + 3, y, z, k), dev(x + 2, y, z, k), partner,
                   dev(x + 1, y, z, 1 - k), dev(x + 3, y, z, 1 - k), dev(x, mate_y, z, k), dev(x + 2, mate_y, z, k)):
        pl.semaphore_signal(barrier, inc=1, device_id=target, device_id_type=pl.DeviceIdType.MESH)

    values = emb[...].astype(F32)
    unit = (values * lax.rsqrt(jnp.sum(values * values, axis=1, keepdims=True) + 1e-06)).astype(BF16)
    lane = cluster[...]
    member = lax.broadcasted_iota(jnp.int32, (N, ROWS), 0) == lane
    upper = lax.broadcasted_iota(jnp.int32, (ROWS, ROWS), 0) < lax.broadcasted_iota(jnp.int32, (ROWS, ROWS), 1)
    before = lax.dot_general(
        member.astype(F32).astype(BF16), upper.astype(F32).astype(BF16), (((1,), (0,)), ((), ())),
        preferred_element_type=F32)
    rank = jnp.sum(jnp.where(member, before, F32(0.0)), axis=0, keepdims=True)
    slot[...] = jnp.broadcast_to(lane.astype(F32) * CAP + rank, (8, ROWS))
    orders = order[...].astype(F32)

    def place(begin, size):
        index = lax.broadcasted_iota(jnp.int32, (size, ROWS), 0).astype(F32) + F32(begin)
        return index == slot[0:1, :]

    ocols = []
    for t in range(4):
        hit = place(t * 192, 192)
        send[t * 192:(t + 1) * 192, :] = lax.dot_general(
            hit.astype(F32).astype(BF16), unit, (((1,), (0,)), ((), ())), preferred_element_type=F32).astype(BF16)
        ocols.append(jnp.broadcast_to(
            jnp.min(jnp.where(hit, orders, F32(BIG)), axis=1, keepdims=True), (192, 128)))
    osend[...] = jnp.broadcast_to(to_rows(jnp.concatenate(ocols, axis=0))[:, None, :], (N, 8, 128))
    rowacc[...] = jnp.full((6, S, 128), -1.0, F32)
    colacc[...] = jnp.full((7, 8, S), -1.0, F32)

    pl.semaphore_wait(barrier, N - 1 + 8)

    mine = (y // 2) * NZ + z
    own_rows = pltpu.make_async_copy(send.at[chunk(mine)], buf.at[0, chunk(0)], d_recv.at[0, 0])
    own_rows.start()
    own_order = pltpu.make_async_copy(osend.at[mine], orecv.at[0], local.at[0])
    own_order.start()

    def deal(n):
        target, c, _ = route(n)
        remote(send.at[chunk(c)], buf.at[0, chunk(n)], d_send.at[0], d_recv.at[0, n], target).start()

    def deal_order(n):
        target, c, _ = route(n)
        remote(osend.at[c], orecv.at[n], oc_send, oc_recv, target).start()

    via = dev(x, y, (z + NZ - 2) % NZ, k)

    def deal_far(n):
        target, c, _ = route(n)

        @pl.when(k == 0)
        def _():
            remote(send.at[chunk(c)], buf.at[0, chunk(n)], d_send.at[0], d_recv.at[0, n], target).start()

        @pl.when(k == 1)
        def _():
            remote(send.at[chunk(c)], mid.at[chunk(n - 14)], d_send.at[0], m_recv.at[n - 14], via).start()

    def pass_on(n):
        yy = (n % 2) * (NY - 1 - y) + (1 - n % 2) * y
        pltpu.make_async_copy(mid.at[chunk(n - 14)], mid.at[chunk(n - 14)], m_recv.at[n - 14]).wait()
        remote(mid.at[chunk(n - 14)], buf.at[0, chunk(n)], m_send, d_recv.at[0, n],
               dev(x, yy, (z + NZ - 2) % NZ, k)).start()

    for n in range(1, N):
        deal_order(n)
    for n in (1, 2, 3, 4, 5, 6, 7, 8, 9, 14, 15, 10, 11, 12, 13):
        if n < 14:
            deal(n)
        else:
            deal_far(n)

    def relay(source, n, block, target):
        return remote(buf.at[source, chunk(n)], buf.at[block, chunk(n)], d_send.at[block], d_recv.at[block, n], target)

    def arrived(block, n):
        pltpu.make_async_copy(buf.at[block, chunk(n)], buf.at[block, chunk(n)], d_recv.at[block, n]).wait()

    all_but_one = pl.ds(1, N - 1)

    def share_orders():
        own_order.wait()
        remote(osend.at[all_but_one], orecv.at[all_but_one], oc_send, oc_recv, partner).wait()
        oblk[0] = jnp.max(orecv[...], axis=1)
        for b in range(1, 6):
            remote(oblk.at[0], oblk.at[b], ob_send.at[b], ob_recv.at[b], users[b]).start()

    def spread_orders(b, carry):
        column = to_column(oblk[b])
        ocol[b] = column
        olane[b] = jnp.transpose(column)[0:8, :]
        return carry

    def take_orders():
        for b in range(1, 6):
            remote(oblk.at[0], oblk.at[b], ob_send.at[b], ob_recv.at[b], users[b]).wait()
        lax.fori_loop(0, 6, spread_orders, 0)

    def drain(begin, end):
        for b in range(3, 6):
            def one(n, carry, b=b):
                arrived(b, n)
                return carry

            lax.fori_loop(begin, end, one, 0)

    def pair(v):
        u = v - 1
        real = (v + 9) // 10
        g1, g2 = (u + 5) // 7, u // 7
        i = (3 * (g1 - g2) + (2 + 2 * k) * g2) * real
        j = ((1 - g1) * (1 + u) + (g1 - g2) * (u - 3 + (u + 1) // 3) + g2 * (u - 3 - 4 * k)) * real
        return i, j, j + 6 * (1 - real)

    def compare(i, j, to, begin, size, c):
        rows = pl.ds(begin, size)
        cols = pl.ds(pl.multiple_of(c * 256, 256), 256)
        score = lax.dot_general(
            buf[i, rows, :], buf[j, cols, :], (((1,), (1,)), ((), ())), preferred_element_type=F32)
        earlier = olane[j, 0:1, cols] < jnp.concatenate([ocol[i, rows, :]] * 2, axis=1)
        seen = jnp.where(earlier, score, F32(-1.0))
        rowacc[i, rows, :] = jnp.maximum(rowacc[i, rows, :], jnp.maximum(seen[:, 0:128], seen[:, 128:256]))
        other = jnp.where(earlier, F32(-1.0), score)
        colacc[to, :, cols] = jnp.maximum(
            colacc[to, :, cols], jnp.max(other.reshape(size // 8, 8, 256), axis=0))

    def tile(v, r, c):
        i, j, to = pair(v)
        compare(i, j, to, pl.multiple_of(r * 256, 256), 256, c)

    def first(v, carry):
        tile(v, 0, 0)
        return carry

    gap = 2 * LAG

    def step(n, carry):
        @pl.when(n < N)
        def _():
            arrived(0, n)
            relay(0, n, 1, users[1]).start()
            relay(0, n, 4, users[4]).start()

        @pl.when(jnp.logical_and(n >= LAG, n < N + LAG))
        def _():
            m = n - LAG
            arrived(1, m)
            relay(1, m, 2, users[1]).start()
            relay(1, m, 5, users[4]).start()

        @pl.when(jnp.logical_and(n >= gap, n < N + gap))
        def _():
            m = n - gap
            arrived(2, m)
            relay(2 * k, m, 3, dev(x, mate_y, z, k)).start()

        @pl.when(n == 6)
        def _():
            share_orders()

        @pl.when(jnp.logical_and(n == 8, k == 1))
        def _():
            pass_on(14)
            pass_on(15)

        @pl.when(n == 10)
        def _():
            take_orders()

        @pl.when(n == 11)
        def _():
            drain(0, 6)

        @pl.when(jnp.logical_and(n >= 11, n < 14))
        def _():
            lax.fori_loop((n - 11) * 3, (n - 11) * 3 + 3 + n // 13, first, 0)

        @pl.when(n == 17)
        def _():
            drain(6, 11)

        @pl.when(n >= 14)
        def _():
            def second(q, carry):
                tile(n - 14, 1 - q % 2, (q + 1) // 2)
                return carry

            lax.fori_loop(0, 3, second, 0)

        return carry

    lax.fori_loop(0, 24, step, 0)
    drain(11, N)

    side_x, side_y = 1 - x // 2, 1 - y % 2

    def third(v, carry):
        i, j, to = pair(v)
        shared = jnp.logical_or(jnp.logical_or(v == 2, v == 3), v == 5)
        lead = jnp.where(v == 2, side_x, jnp.where(v == 3, side_y, 1 - side_y))

        @pl.when(jnp.logical_or(jnp.logical_not(shared), lead == 1))
        def _():
            compare(i, j, to, 0, 768, 2)

        @pl.when(jnp.logical_not(shared))
        def _():
            compare(j, i, i, 0, 512, 2)

        @pl.when(jnp.logical_and(shared, lead == 0))
        def _():
            compare(i, j, j, 0, 512, 2)

        return carry

    lax.fori_loop(0, 10, third, 0)

    def collect(b, carry):
        column = jnp.max(rowacc[b], axis=1, keepdims=True)
        line = jnp.max(colacc[b], axis=0, keepdims=True)
        both = jnp.maximum(column, jnp.transpose(jnp.broadcast_to(line, (128, S))))
        res[b] = to_rows(both)
        return carry

    lax.fori_loop(0, 6, collect, 0)
    for b in range(1, 6):
        remote(res.at[b], rrecv.at[b], r_send.at[b], r_recv.at[b], homes[b]).start()
    rrecv[0] = res[0]
    for b in range(1, 6):
        remote(res.at[b], rrecv.at[b], r_send.at[b], r_recv.at[b], homes[b]).wait()
    best = jnp.max(rrecv[...], axis=0)
    fsend[...] = jnp.broadcast_to(best[:, None, :], (N, 8, 128))

    own_best = pltpu.make_async_copy(fsend.at[0], fin.at[mine], local.at[1])
    own_best.start()

    def give_back(n, carry):
        remote(fsend.at[n], fin.at[mine], f_send, f_recv, route(n)[2]).start()
        return carry

    lax.fori_loop(1, N, give_back, 0)
    remote(buf.at[0, pl.ds(0, S - CAP)], buf.at[0, pl.ds(0, S - CAP)], d_send.at[0], d_recv.at[0, 0], partner).wait_send()
    for b in range(1, 6):
        remote(buf.at[b], buf.at[b], d_send.at[b], d_recv.at[b, 0], partner).wait_send()
    @pl.when(k == 1)
    def _():
        pltpu.make_async_copy(mid, mid, m_send).wait()

    own_best.wait()
    remote(fsend.at[all_but_one], fin.at[all_but_one], f_send, f_recv, partner).wait()
    column = to_column(jnp.max(fin[...], axis=1))
    total = jnp.full((8, ROWS), -BIG, F32)
    for t in range(4):
        hit = place(t * 192, 192)
        part = jnp.where(hit, jnp.concatenate([column[t * 192:(t + 1) * 192, :]] * 4, axis=1), F32(-BIG))
        total = jnp.maximum(total, jnp.max(part.reshape(24, 8, ROWS), axis=0))
    out[...] = jnp.max(total, axis=0, keepdims=True)


def on_device(embeddings, cluster_ids, row_order):
    vmem = pl.BlockSpec(memory_space=pltpu.VMEM)
    dma = pltpu.SemaphoreType.DMA
    result = pl.pallas_call(
        kernel,
        out_shape=jax.ShapeDtypeStruct((1, ROWS), F32),
        in_specs=[vmem] * 3,
        out_specs=vmem,
        scratch_shapes=[
            pltpu.VMEM((S, D), BF16),
            pltpu.VMEM((6, S, D), BF16),
            pltpu.VMEM((8, ROWS), F32),
            pltpu.VMEM((N, 8, 128), F32),
            pltpu.VMEM((N, 8, 128), F32),
            pltpu.VMEM((6, N, 128), F32),
            pltpu.VMEM((6, S, 128), F32),
            pltpu.VMEM((6, 8, S), F32),
            pltpu.VMEM((6, S, 128), F32),
            pltpu.VMEM((7, 8, S), F32),
            pltpu.VMEM((6, N, 128), F32),
            pltpu.VMEM((6, N, 128), F32),
            pltpu.VMEM((N, 8, 128), F32),
            pltpu.VMEM((N, 8, 128), F32),
            pltpu.VMEM((2 * CAP, D), BF16),
            dma((2,)), dma, dma((2,)), dma((6,)), dma((6, N)), dma, dma, dma((6,)), dma((6,)), dma((6,)), dma((6,)), dma, dma,
        ],
        compiler_params=pltpu.CompilerParams(
            collective_id=0, has_side_effects=True, vmem_limit_bytes=60 * 1024 * 1024),
    )(embeddings, cluster_ids.reshape(1, ROWS), row_order.reshape(1, ROWS))
    return result.reshape(ROWS)


def solution(mesh):
    spec = P(("bulk", "grp"))
    return jax.shard_map(
        on_device,
        mesh=mesh,
        in_specs=(P(("bulk", "grp"), None), P(("bulk", "grp"), None), spec),
        out_specs=spec,
        check_vma=False,
    )
```

```python
import functools

import jax
import jax.numpy as jnp
from jax import lax
from jax.experimental import pallas as pl
from jax.experimental.pallas import tpu as pltpu
from jax.sharding import PartitionSpec as P

CAP = 48
NX, NY, NZ = 4, 4, 8
N = 16
S = N * CAP
ROWS = 512
D = 768
BIG = 1e9
LAG = 2
F32 = jnp.float32
BF16 = jnp.bfloat16


def diag():
    return lax.broadcasted_iota(jnp.int32, (CAP, 128), 0) == lax.broadcasted_iota(jnp.int32, (CAP, 128), 1)


def to_rows(column):
    parts = column.reshape(N, CAP, 128)
    return jnp.max(jnp.where(diag()[None], parts, F32(-BIG)), axis=1)


def to_column(rows):
    parts = jnp.broadcast_to(rows[:, None, :], (N, CAP, 128))
    value = jnp.max(jnp.where(diag()[None], parts, F32(-BIG)), axis=2, keepdims=True)
    return jnp.broadcast_to(value, (N, CAP, 128)).reshape(S, 128)


def chunk(n):
    return pl.ds(pl.multiple_of(n * CAP, 16), CAP)


def kernel(emb, cluster, order, out,
           send, buf, slot, osend, orecv, oblk, ocol, olane, rowacc, colacc, res, rrecv, fsend, fin,
           mid, local, m_send, m_recv, d_send, d_recv, oc_send, oc_recv, ob_send, ob_recv, r_send, r_recv, f_send, f_recv):
    bulk, grp = lax.axis_index("bulk"), lax.axis_index("grp")
    x, y = bulk // NY, bulk % NY
    z, k = grp // 2, grp % 2
    sgn = 1 - 2 * k

    def dev(xx, yy, zz, kk):
        return (xx % NX) * NY + yy, zz * 2 + kk

    def remote(src, dst, s_sem, r_sem, target):
        return pltpu.make_async_remote_copy(
            src_ref=src, dst_ref=dst, send_sem=s_sem, recv_sem=r_sem,
            device_id=target, device_id_type=pl.DeviceIdType.MESH)

    x_one = dev(x + sgn + NX, y, z, k)
    mate_y = y + 1 - 2 * (y % 2)
    partner = dev(x, y, z, 1 - k)
    homes = [
        None,
        dev(x - sgn + NX, y, z, k),
        dev(x + 2, y, z, k),
        dev(x + 2 * k, mate_y, z, k),
        partner,
        dev(x + sgn + NX, y, z, 1 - k),
    ]
    users = [
        None,
        x_one,
        dev(x + 2, y, z, k),
        dev(x + 2 * k, mate_y, z, k),
        partner,
        dev(x + sgn + NX, y, z, 1 - k),
    ]

    def route(n):
        i, half = n // 2, n % 2
        dz = (i % 2) * ((i + 1) // 2) + (1 - i % 2) * (NZ - i // 2)
        yy = half * (NY - 1 - y) + (1 - half) * y
        zz = (z + dz) % NZ
        return dev(x, yy, zz, k), (yy // 2) * NZ + zz, dev(x, yy, (z - dz + 2 * NZ) % NZ, k)

    barrier = pltpu.get_barrier_semaphore()

    def greet(n, carry):
        pl.semaphore_signal(barrier, inc=1, device_id=route(n)[0], device_id_type=pl.DeviceIdType.MESH)
        return carry

    lax.fori_loop(1, N, greet, 0)
    for target in (dev(x + 1, y, z, k), dev(x + 3, y, z, k), dev(x + 2, y, z, k), partner,
                   dev(x + 1, y, z, 1 - k), dev(x + 3, y, z, 1 - k), dev(x, mate_y, z, k), dev(x + 2, mate_y, z, k)):
        pl.semaphore_signal(barrier, inc=1, device_id=target, device_id_type=pl.DeviceIdType.MESH)

    values = emb[...].astype(F32)
    unit = (values * lax.rsqrt(jnp.sum(values * values, axis=1, keepdims=True) + 1e-06)).astype(BF16)
    lane = cluster[...]
    member = lax.broadcasted_iota(jnp.int32, (N, ROWS), 0) == lane
    upper = lax.broadcasted_iota(jnp.int32, (ROWS, ROWS), 0) < lax.broadcasted_iota(jnp.int32, (ROWS, ROWS), 1)
    before = lax.dot_general(
        member.astype(F32).astype(BF16), upper.astype(F32).astype(BF16), (((1,), (0,)), ((), ())),
        preferred_element_type=F32)
    rank = jnp.sum(jnp.where(member, before, F32(0.0)), axis=0, keepdims=True)
    slot[...] = jnp.broadcast_to(lane.astype(F32) * CAP + rank, (8, ROWS))
    orders = order[...].astype(F32)

    def place(begin, size):
        index = lax.broadcasted_iota(jnp.int32, (size, ROWS), 0).astype(F32) + F32(begin)
        return index == slot[0:1, :]

    ocols = []
    for t in range(4):
        hit = place(t * 192, 192)
        send[t * 192:(t + 1) * 192, :] = lax.dot_general(
            hit.astype(F32).astype(BF16), unit, (((1,), (0,)), ((), ())), preferred_element_type=F32).astype(BF16)
        ocols.append(jnp.broadcast_to(
            jnp.min(jnp.where(hit, orders, F32(BIG)), axis=1, keepdims=True), (192, 128)))
    osend[...] = jnp.broadcast_to(to_rows(jnp.concatenate(ocols, axis=0))[:, None, :], (N, 8, 128))
    rowacc[...] = jnp.full((6, S, 128), -1.0, F32)
    colacc[...] = jnp.full((7, 8, S), -1.0, F32)

    pl.semaphore_wait(barrier, N - 1 + 8)

    mine = (y // 2) * NZ + z
    own_rows = pltpu.make_async_copy(send.at[chunk(mine)], buf.at[0, chunk(0)], d_recv.at[0, 0])
    own_rows.start()
    own_order = pltpu.make_async_copy(osend.at[mine], orecv.at[0], local.at[0])
    own_order.start()

    def deal(n):
        target, c, _ = route(n)
        remote(send.at[chunk(c)], buf.at[0, chunk(n)], d_send.at[0], d_recv.at[0, n], target).start()

    def deal_order(n):
        target, c, _ = route(n)
        remote(osend.at[c], orecv.at[n], oc_send, oc_recv, target).start()

    via = dev(x, y, (z + NZ - 2) % NZ, k)

    def deal_far(n):
        target, c, _ = route(n)

        @pl.when(k == 0)
        def _():
            remote(send.at[chunk(c)], buf.at[0, chunk(n)], d_send.at[0], d_recv.at[0, n], target).start()

        @pl.when(k == 1)
        def _():
            remote(send.at[chunk(c)], mid.at[chunk(n - 14)], d_send.at[0], m_recv.at[n - 14], via).start()

    def pass_on(n):
        yy = (n % 2) * (NY - 1 - y) + (1 - n % 2) * y
        pltpu.make_async_copy(mid.at[chunk(n - 14)], mid.at[chunk(n - 14)], m_recv.at[n - 14]).wait()
        remote(mid.at[chunk(n - 14)], buf.at[0, chunk(n)], m_send, d_recv.at[0, n],
               dev(x, yy, (z + NZ - 2) % NZ, k)).start()

    for n in range(1, N):
        deal_order(n)
    for n in (1, 2, 3, 4, 5, 6, 7, 8, 9, 14, 15, 10, 11, 12, 13):
        if n < 14:
            deal(n)
        else:
            deal_far(n)

    def relay(source, n, block, target):
        return remote(buf.at[source, chunk(n)], buf.at[block, chunk(n)], d_send.at[block], d_recv.at[block, n], target)

    def arrived(block, n):
        pltpu.make_async_copy(buf.at[block, chunk(n)], buf.at[block, chunk(n)], d_recv.at[block, n]).wait()

    all_but_one = pl.ds(1, N - 1)

    def share_orders():
        own_order.wait()
        remote(osend.at[all_but_one], orecv.at[all_but_one], oc_send, oc_recv, partner).wait()
        oblk[0] = jnp.max(orecv[...], axis=1)
        for b in range(1, 6):
            remote(oblk.at[0], oblk.at[b], ob_send.at[b], ob_recv.at[b], users[b]).start()

    def spread_orders(b, carry):
        column = to_column(oblk[b])
        ocol[b] = column
        olane[b] = jnp.transpose(column)[0:8, :]
        return carry

    def take_orders():
        for b in range(1, 6):
            remote(oblk.at[0], oblk.at[b], ob_send.at[b], ob_recv.at[b], users[b]).wait()
        lax.fori_loop(0, 6, spread_orders, 0)

    def drain(begin, end):
        for b in range(3, 6):
            def one(n, carry, b=b):
                arrived(b, n)
                return carry

            lax.fori_loop(begin, end, one, 0)

    def pair(v):
        u = v - 1
        real = (v + 9) // 10
        g1, g2 = (u + 5) // 7, u // 7
        i = (3 * (g1 - g2) + (2 + 2 * k) * g2) * real
        j = ((1 - g1) * (1 + u) + (g1 - g2) * (u - 3 + (u + 1) // 3) + g2 * (u - 3 - 4 * k)) * real
        return i, j, j + 6 * (1 - real)

    def compare(i, j, to, begin, size, c):
        rows = pl.ds(begin, size)
        cols = pl.ds(pl.multiple_of(c * 256, 256), 256)
        score = lax.dot_general(
            buf[i, rows, :], buf[j, cols, :], (((1,), (1,)), ((), ())), preferred_element_type=F32)
        earlier = olane[j, 0:1, cols] < jnp.concatenate([ocol[i, rows, :]] * 2, axis=1)
        seen = jnp.where(earlier, score, F32(-1.0))
        rowacc[i, rows, :] = jnp.maximum(rowacc[i, rows, :], jnp.maximum(seen[:, 0:128], seen[:, 128:256]))
        other = jnp.where(earlier, F32(-1.0), score)
        colacc[to, :, cols] = jnp.maximum(
            colacc[to, :, cols], jnp.max(other.reshape(size // 8, 8, 256), axis=0))

    def tile(v, r, c):
        i, j, to = pair(v)
        compare(i, j, to, pl.multiple_of(r * 256, 256), 256, c)

    def first(v, carry):
        tile(v, 0, 0)
        return carry

    def second(v, carry):
        i, j, to = pair(v)
        compare(i, j, to, 0, 512, 1)
        compare(j, i, i, 0, 256, 1)
        return carry

    gap = 2 * LAG

    def step(n, carry):
        @pl.when(n < N)
        def _():
            arrived(0, n)
            relay(0, n, 1, users[1]).start()
            relay(0, n, 4, users[4]).start()

        @pl.when(jnp.logical_and(n >= LAG, n < N + LAG))
        def _():
            m = n - LAG
            arrived(1, m)
            relay(1, m, 2, users[1]).start()
            relay(1, m, 5, users[4]).start()

        @pl.when(jnp.logical_and(n >= gap, n < N + gap))
        def _():
            m = n - gap
            arrived(2, m)
            relay(2 * k, m, 3, dev(x, mate_y, z, k)).start()

        @pl.when(n == 6)
        def _():
            share_orders()

        @pl.when(jnp.logical_and(n == 8, k == 1))
        def _():
            pass_on(14)
            pass_on(15)

        @pl.when(n == 10)
        def _():
            take_orders()

        @pl.when(n == 11)
        def _():
            drain(0, 6)

        @pl.when(jnp.logical_and(n >= 11, n < 14))
        def _():
            lax.fori_loop((n - 11) * 3, (n - 11) * 3 + 3 + n // 13, first, 0)

        @pl.when(n == 16)
        def _():
            drain(6, 11)

        @pl.when(n >= 14)
        def _():
            m = n - 14
            lax.fori_loop(2 * m - jnp.minimum(m, 1), jnp.minimum(2 * m + 1, 10), second, 0)

        return carry

    lax.fori_loop(0, N + gap, step, 0)
    drain(11, N)

    side_x, side_y = 1 - x // 2, 1 - y % 2

    def third(v, carry):
        i, j, to = pair(v)
        shared = jnp.logical_or(jnp.logical_or(v == 2, v == 3), v == 5)
        lead = jnp.where(v == 2, side_x, jnp.where(v == 3, side_y, 1 - side_y))

        @pl.when(jnp.logical_or(jnp.logical_not(shared), lead == 1))
        def _():
            compare(i, j, to, 0, 768, 2)

        @pl.when(jnp.logical_not(shared))
        def _():
            compare(j, i, i, 0, 512, 2)

        @pl.when(jnp.logical_and(shared, lead == 0))
        def _():
            compare(i, j, j, 0, 512, 2)

        return carry

    def most(t, carry):
        return third(t + 3 - (t // 7) * (2 * t - 6), carry)

    lax.fori_loop(0, 9, most, 0)

    def collect(b, carry):
        column = jnp.max(rowacc[b], axis=1, keepdims=True)
        line = jnp.max(colacc[b], axis=0, keepdims=True)
        both = jnp.maximum(column, jnp.transpose(jnp.broadcast_to(line, (128, S))))
        res[b] = to_rows(both)
        return carry

    lax.fori_loop(1, 6, collect, 0)
    for b in range(1, 6):
        remote(res.at[b], rrecv.at[b], r_send.at[b], r_recv.at[b], homes[b]).start()
    third(0, 0)
    collect(0, 0)
    rrecv[0] = res[0]
    for b in range(1, 6):
        remote(res.at[b], rrecv.at[b], r_send.at[b], r_recv.at[b], homes[b]).wait()
    best = jnp.max(rrecv[...], axis=0)
    fsend[...] = jnp.broadcast_to(best[:, None, :], (N, 8, 128))

    own_best = pltpu.make_async_copy(fsend.at[0], fin.at[mine], local.at[1])
    own_best.start()

    def give_back(n, carry):
        remote(fsend.at[n], fin.at[mine], f_send, f_recv, route(n)[2]).start()
        return carry

    lax.fori_loop(1, N, give_back, 0)
    remote(buf.at[0, pl.ds(0, S - CAP)], buf.at[0, pl.ds(0, S - CAP)], d_send.at[0], d_recv.at[0, 0], partner).wait_send()
    for b in range(1, 6):
        remote(buf.at[b], buf.at[b], d_send.at[b], d_recv.at[b, 0], partner).wait_send()
    @pl.when(k == 1)
    def _():
        pltpu.make_async_copy(mid, mid, m_send).wait()

    own_best.wait()
    remote(fsend.at[all_but_one], fin.at[all_but_one], f_send, f_recv, partner).wait()
    column = to_column(jnp.max(fin[...], axis=1))
    total = jnp.full((8, ROWS), -BIG, F32)
    for t in range(4):
        hit = place(t * 192, 192)
        part = jnp.where(hit, jnp.concatenate([column[t * 192:(t + 1) * 192, :]] * 4, axis=1), F32(-BIG))
        total = jnp.maximum(total, jnp.max(part.reshape(24, 8, ROWS), axis=0))
    out[...] = jnp.max(total, axis=0, keepdims=True)


def on_device(embeddings, cluster_ids, row_order):
    vmem = pl.BlockSpec(memory_space=pltpu.VMEM)
    dma = pltpu.SemaphoreType.DMA
    result = pl.pallas_call(
        kernel,
        out_shape=jax.ShapeDtypeStruct((1, ROWS), F32),
        in_specs=[vmem] * 3,
        out_specs=vmem,
        scratch_shapes=[
            pltpu.VMEM((S, D), BF16),
            pltpu.VMEM((6, S, D), BF16),
            pltpu.VMEM((8, ROWS), F32),
            pltpu.VMEM((N, 8, 128), F32),
            pltpu.VMEM((N, 8, 128), F32),
            pltpu.VMEM((6, N, 128), F32),
            pltpu.VMEM((6, S, 128), F32),
            pltpu.VMEM((6, 8, S), F32),
            pltpu.VMEM((6, S, 128), F32),
            pltpu.VMEM((7, 8, S), F32),
            pltpu.VMEM((6, N, 128), F32),
            pltpu.VMEM((6, N, 128), F32),
            pltpu.VMEM((N, 8, 128), F32),
            pltpu.VMEM((N, 8, 128), F32),
            pltpu.VMEM((2 * CAP, D), BF16),
            dma((2,)), dma, dma((2,)), dma((6,)), dma((6, N)), dma, dma, dma((6,)), dma((6,)), dma((6,)), dma((6,)), dma, dma,
        ],
        compiler_params=pltpu.CompilerParams(
            collective_id=0, has_side_effects=True, vmem_limit_bytes=60 * 1024 * 1024),
    )(embeddings, cluster_ids.reshape(1, ROWS), row_order.reshape(1, ROWS))
    return result.reshape(ROWS)


def solution(mesh):
    spec = P(("bulk", "grp"))
    return jax.shard_map(
        on_device,
        mesh=mesh,
        in_specs=(P(("bulk", "grp"), None), P(("bulk", "grp"), None), spec),
        out_specs=spec,
        check_vma=False,
    )
```
